32 devices in a mesh: expert: 16 (over z, x, core), replica: 2 (over y).
Axes of the slice: x: 2, y: 2, z: 4, core: 2. Of those that a mesh axis runs over, the one named last changes fastest.
Arguments:
- tokens: bfloat16 [192, 3584], P('expert', 'replica'), may hold values from -6 to 6
- expert_ids: int32 [192, 8], P('expert'), may hold values from 0 to 7, all different within a row; in each aligned block of 12 rows (0 to 11, 12 to 23, ...) at most 12 rows name the same one
- gate_values: float32 [192, 8], P('expert'), may hold values from 0.1 to 0.6
- gate_weight: bfloat16 [16, 512, 3584], P('expert', 'replica'), may hold values from -0.09375 to 0.09375
- up_weight: bfloat16 [16, 512, 3584], P('expert', 'replica'), may hold values from -0.09375 to 0.09375
- down_weight: bfloat16 [16, 512, 3584], P('expert', None, 'replica'), may hold values from -0.1875 to 0.1875
- out_grad: bfloat16 [192, 3584], P('expert', 'replica'), may hold values from -1.5 to 1.5
Outputs:
- moe_out: bfloat16 [192, 3584], P('expert', 'replica')
- token_grad: bfloat16 [192, 3584], P('expert', 'replica')
- gate_grad: bfloat16 [16, 512, 3584], P('expert', 'replica')
- up_grad: bfloat16 [16, 512, 3584], P('expert', 'replica')
- down_grad: bfloat16 [16, 512, 3584], P('expert', None, 'replica')
The draws below stay inside these ranges and needn't reach their ends.
Inputs may be any that keep to these rules, and one draw needn't show every extreme that they name: `expert_ids`: each row names 8 different experts. Among the 12 rows of one index of expert, no expert is named by more than 12 rows, a bound that some block reaches.
All inputs are finite; a program needn't handle non-finite values.
Results may differ from the reference program's by a relative error of at most 0.0075.
Values may be sent and summed in bfloat16 or wider, within the bound.
No kernel may reach another device: no remote copies, remote signals or barrier semaphores. Data moves between devices by JAX's collectives and lax.ppermute only.
A program may use at most 128 MiB of HBM per device.

```python
import math
import jax
import jax.numpy as jnp
import numpy as np
from jax import lax

D = 3584
FF = 1024
TOPK = 8
TOK_DEV = 12
EXPERTS = 8
TOKENS = 192
MOST = 12
N_EXPERT = 16


def level_of(stream_key, shape, pieces, smallest, high):
    loudness, own = 1.0, jax.random.fold_in(stream_key, 6)
    for axis_at, parts in pieces:
        heights = jnp.exp(jax.random.uniform(jax.random.fold_in(own, axis_at), (parts,), jnp.float32, smallest / len(pieces), high / len(pieces)))
        loudness = loudness * jnp.repeat(heights, shape[axis_at] // parts).reshape([-1 if axis == axis_at else 1 for axis in range(len(shape))])
    return loudness


def routed_block(own_key, own, number, rows, number_of, top, reach, skew):
    ranking = jax.random.permutation(own_key, number_of)
    heavy_load, usual = shares(number_of, rows * top, reach, skew, True), shares(number_of, rows * top, reach, skew, False)
    places = jnp.arange(number_of)

    def named(sizes, turn):
        used = int((sizes > 0).sum())
        fixed = max(1, used // 4)
        shifted = fixed + (places - fixed + turn * (used - fixed)) % max(1, number_of - fixed)
        return jnp.zeros((number_of,), jnp.int32).at[ranking[jnp.where(places < fixed, places, shifted)]].set(jnp.asarray(sizes, jnp.int32))

    sizes = jnp.where(number % 4 == 0, named(heavy_load, number // 4), named(usual, number - number // 4 - 1))
    mixed = jax.random.permutation(jax.random.fold_in(own, 3), number_of)
    donor, taker = mixed[0:number_of // 2 * 2:2], mixed[1:number_of // 2 * 2:2]
    slack = jnp.minimum(sizes[donor] - 1, reach - sizes[taker]) // 2
    slack = jnp.where((donor == ranking[0]) | (taker == ranking[0]) | (sizes[taker] == 0), 0, jnp.maximum(slack, 0))
    shifted = jax.random.randint(jax.random.fold_in(own, 4), (number_of // 2,), 0, 1 << 20) % (slack + 1)
    sizes = sizes.at[donor].add(-shifted).at[taker].add(shifted)
    labels = jnp.searchsorted(jnp.cumsum(sizes), jnp.arange(rows * top), side="right").astype(jnp.int32)
    table = labels.reshape(top, rows).T
    table = table[jax.random.permutation(jax.random.fold_in(own, 1), rows)]
    turn = jax.random.randint(jax.random.fold_in(own, 2), (rows, 1), 0, top)
    return jnp.take_along_axis(table, (jnp.arange(top)[None, :] + turn) % top, axis=1)


def shares(amount, total, bound, slope, full):
    weights = [(1 << 20) // math.isqrt(grade ** slope) + 1 for grade in range(1, amount + 1)]
    largest = bound if full else min(bound, max(-(-total // amount), total * weights[0] // sum(weights)))
    least = 1 if total - largest >= amount - 1 else 0
    counts, rest = [largest] + [least] * (amount - 1), total - largest - least * (amount - 1)
    while rest > 0:
        candidates = [i for i in range(1, amount) if counts[i] < largest] or [i for i in range(1, amount) if counts[i] < bound]
        pool, budget = sum([weights[i] for i in candidates]), rest
        for i in candidates:
            addition = min(bound - counts[i], max(1, budget * weights[i] // pool), rest)
            counts[i] = counts[i] + addition
            rest = rest - addition
    return np.array(counts)


def gaussian(rng, extent, width, bound, split=(), kind=jnp.bfloat16):
    loudness = level_of(rng, extent, split, -0.22, 0.18) if split else 1.0
    entries = jax.random.normal(rng, extent, jnp.float32) * width * loudness
    return jnp.minimum(jnp.maximum(entries, -bound), bound).astype(kind)


def setup_inputs(seed: int = 0) -> dict:
    streams_of = jax.random.split(jax.random.key(seed), 8)
    tokens = gaussian(streams_of[0], (TOKENS, D), 1.0, 6.0, ((0, 16), (1, 2)))
    expert_ids_keys = jax.random.split(jax.random.fold_in(streams_of[1], 1), TOKENS // TOK_DEV)
    expert_ids_turns = jax.random.permutation(jax.random.fold_in(streams_of[1], 3), TOKENS // TOK_DEV)
    expert_ids = jax.vmap(lambda own, number: routed_block(jax.random.fold_in(streams_of[1], 2), own, number, TOK_DEV, EXPERTS, TOPK, MOST, 1))(expert_ids_keys, expert_ids_turns).reshape((TOKENS, TOPK))
    gate_values = jnp.clip(0.1 + 0.5 * jax.random.uniform(streams_of[2], (TOKENS, TOPK), jnp.float32) ** level_of(streams_of[2], (TOKENS, TOPK), ((0, 16),), -0.2, 0.2), 0.1, 0.6)
    gate_weight = gaussian(streams_of[3], (N_EXPERT, FF // 2, D), D ** -0.5, 0.09375, ((0, 16), (1, 2)))
    up_weight = gaussian(streams_of[4], (N_EXPERT, FF // 2, D), D ** -0.5, 0.09375, ((0, 16), (1, 2)))
    down_weight = gaussian(streams_of[5], (N_EXPERT, FF // 2, D), FF ** -0.5, 0.1875, ((0, 16), (2, 2)))
    out_grad = gaussian(streams_of[6], (TOKENS, D), 0.25, 1.5, ((0, 16), (1, 2)))
    return {"tokens": tokens, "expert_ids": expert_ids, "gate_values": gate_values, "gate_weight": gate_weight, "up_weight": up_weight, "down_weight": down_weight, "out_grad": out_grad}


def reference(tokens, expert_ids, gate_values, gate_weight, up_weight, down_weight, out_grad):
    pair_count = TOKENS * TOPK
    room_size = N_EXPERT * MOST
    flat_ids = expert_ids.reshape(pair_count).astype(jnp.int32)
    onehot = (flat_ids[:, None] == jnp.arange(EXPERTS, dtype=jnp.int32)[None, :]).astype(jnp.int32)
    rank_in = jnp.sum((jnp.cumsum(onehot, axis=0) - onehot) * onehot, axis=1).astype(jnp.int32)
    place = (flat_ids * room_size + rank_in).astype(jnp.int32)
    source_pair = jnp.zeros((EXPERTS * room_size,), jnp.int32).at[place].set(jnp.arange(pair_count, dtype=jnp.int32))
    filled = jnp.zeros((EXPERTS * room_size,), jnp.float32).at[place].set(1.0)
    token_index = (source_pair // TOPK).astype(jnp.int32).reshape(EXPERTS, room_size)
    live_mask = filled.reshape(EXPERTS, room_size)
    weight_of = gate_values.reshape(pair_count)[source_pair].reshape(EXPERTS, room_size)
    gate_mats = jnp.swapaxes(jnp.concatenate([gate_weight[0::2], gate_weight[1::2]], axis=1), 1, 2)
    up_mats = jnp.swapaxes(jnp.concatenate([up_weight[0::2], up_weight[1::2]], axis=1), 1, 2)
    down_mats = jnp.concatenate([down_weight[0::2], down_weight[1::2]], axis=1)

    def one_expert(operands):
        rows_index, row_live, row_weight, gate_mat, up_mat, down_mat = operands
        rows_in = jnp.where(row_live[:, None] > 0, tokens[rows_index], jnp.zeros((), tokens.dtype))
        pre_gate = jnp.dot(rows_in, gate_mat, preferred_element_type=jnp.float32)
        pre_up = jnp.dot(rows_in, up_mat, preferred_element_type=jnp.float32)
        sigma = jax.nn.sigmoid(pre_gate)
        activated = pre_gate * sigma
        slope_term = sigma * (1.0 + pre_gate * (1.0 - sigma))
        hidden = (activated * pre_up).astype(jnp.bfloat16)
        expert_out = jnp.dot(hidden, down_mat, preferred_element_type=jnp.float32).astype(jnp.bfloat16)
        cotangent = jnp.where(row_live[:, None] > 0, row_weight[:, None] * out_grad[rows_index].astype(jnp.float32), 0.0).astype(jnp.bfloat16)
        down_part = jnp.dot(hidden.T, cotangent, preferred_element_type=jnp.float32)
        hidden_grad = jnp.dot(cotangent, down_mat.T, preferred_element_type=jnp.float32)
        gate_act = (hidden_grad * pre_up * slope_term).astype(jnp.bfloat16)
        up_act = (hidden_grad * activated).astype(jnp.bfloat16)
        gate_part = jnp.dot(rows_in.T, gate_act, preferred_element_type=jnp.float32)
        up_part = jnp.dot(rows_in.T, up_act, preferred_element_type=jnp.float32)
        input_rows = (jnp.dot(gate_act, gate_mat.T, preferred_element_type=jnp.float32) + jnp.dot(up_act, up_mat.T, preferred_element_type=jnp.float32)).astype(jnp.bfloat16)
        return expert_out, input_rows, gate_part.astype(jnp.bfloat16), up_part.astype(jnp.bfloat16), down_part.astype(jnp.bfloat16)

    outs_all, inputs_all, gate_parts, up_parts, down_parts = lax.map(one_expert, (token_index, live_mask, weight_of, gate_mats, up_mats, down_mats))
    picked = outs_all.reshape(EXPERTS * room_size, D)[place].astype(jnp.float32).reshape(TOKENS, TOPK, D)
    moe_out = jnp.sum(picked * gate_values[:, :, None], axis=1).astype(jnp.bfloat16)
    picked_grad = inputs_all.reshape(EXPERTS * room_size, D)[place].astype(jnp.float32).reshape(TOKENS, TOPK, D)
    token_grad = jnp.sum(picked_grad, axis=1).astype(jnp.bfloat16)
    gate_grad = jnp.swapaxes(gate_parts, 1, 2).reshape(N_EXPERT, FF // 2, D)
    up_grad = jnp.swapaxes(up_parts, 1, 2).reshape(N_EXPERT, FF // 2, D)
    down_grad = down_parts.reshape(N_EXPERT, FF // 2, D)
    return moe_out, token_grad, gate_grad, up_grad, down_grad
```

```python
import functools

import jax
import jax.numpy as jnp
from jax import lax
from jax.experimental import pallas as pl
from jax.experimental.pallas import tpu as pltpu
from jax.sharding import PartitionSpec as P

BF16, F32 = jnp.bfloat16, jnp.float32
LANES = 128

def partner_2(block, axis, distance):
    count = lax.axis_size(axis)
    route = []
    for low in range(count):
        high = low | 1 << distance
        if high != low and high < count:
            route += [(low, high), (high, low)]
    return lax.ppermute(block, axis, route)


def pair_join(parity_bit, own_part, peer_part, stack_axis):
    first_part = jnp.where(parity_bit == 0, own_part, peer_part)
    second_part = jnp.where(parity_bit == 0, peer_part, own_part)
    return jnp.stack([first_part, second_part], axis=stack_axis)


def pick_half(parity_bit, stacked, stack_axis):
    lower = jnp.take(stacked, 0, axis=stack_axis)
    higher = jnp.take(stacked, 1, axis=stack_axis)
    return (jnp.where(parity_bit == 0, lower, higher), jnp.where(parity_bit == 0, higher, lower))


def routed_device(tokens, expert_ids, gate_values, gate_weight, up_weight, down_weight, out_grad):
    experts_axis = lax.axis_size("expert")
    tok_rows, slice_width = tokens.shape
    top_count = expert_ids.shape[1]
    expert_count = experts_axis // 2
    most_rows = min(tok_rows, 4 * tok_rows * top_count // (3 * expert_count))
    capacity = (most_rows + 1) // 2
    pair_count = tok_rows * top_count
    slot_count = experts_axis * capacity
    flat_ids = expert_ids.reshape(pair_count)
    onehot = (flat_ids[:, None] == jnp.arange(expert_count, dtype=jnp.int32)[None, :]).astype(
        jnp.int32
    )
    rank_in = jnp.sum((jnp.cumsum(onehot, axis=0) - onehot) * onehot, axis=1)
    upper_copy = (rank_in >= capacity).astype(jnp.int32)
    target = (2 * flat_ids + upper_copy) * capacity + rank_in - upper_copy * capacity
    slot_match = target[None, :] == jnp.arange(slot_count, dtype=jnp.int32)[:, None]
    filled = jnp.any(slot_match, axis=1)
    source_pair = jnp.sum(
        jnp.where(slot_match, jnp.arange(pair_count, dtype=jnp.int32)[None, :], 0), axis=1
    )
    source_token = source_pair // top_count
    flat_gates = gate_values.reshape(pair_count)
    send_rows = jnp.where(filled[:, None], tokens[source_token], jnp.zeros((), tokens.dtype))
    scaled = flat_gates[source_pair][:, None] * out_grad[source_token].astype(jnp.float32)
    send_grads = jnp.where(filled[:, None], scaled, 0.0).astype(jnp.bfloat16)
    got_rows, got_grads = (
        lax.all_to_all(
            send_rows.reshape(experts_axis, capacity, slice_width),
            "expert",
            split_axis=0,
            concat_axis=0,
            tiled=True,
        ),
        lax.all_to_all(
            send_grads.reshape(experts_axis, capacity, slice_width),
            "expert",
            split_axis=0,
            concat_axis=0,
            tiled=True,
        ),
    )
    rows_part = got_rows.reshape(slot_count, slice_width)
    grads_part = got_grads.reshape(slot_count, slice_width)
    parity_bit = lax.axis_index("expert") % 2
    own_pieces = (gate_weight[0], up_weight[0], down_weight[0])
    partner = partner_2((own_pieces[0], own_pieces[1], own_pieces[2]), "expert", 0)
    w_gate = pair_join(parity_bit, own_pieces[0], partner[0], 0)
    w_up = pair_join(parity_bit, own_pieces[1], partner[1], 0)
    w_down = pair_join(parity_bit, own_pieces[2], partner[2], 0)
    _, quarter, model_width = w_gate.shape
    full_rows = lax.all_gather(rows_part, "replica", axis=1, tiled=True)
    contract = (((1,), (1,)), ((), ()))
    pre_gate = lax.dot_general(
        full_rows,
        w_gate.reshape(2 * quarter, model_width),
        contract,
        preferred_element_type=jnp.float32,
    ).reshape(slot_count, 2, quarter)
    pre_up = lax.dot_general(
        full_rows,
        w_up.reshape(2 * quarter, model_width),
        contract,
        preferred_element_type=jnp.float32,
    ).reshape(slot_count, 2, quarter)
    sigma = jax.nn.sigmoid(pre_gate)
    activated = pre_gate * sigma
    slope_term = sigma * (1.0 + pre_gate * (1.0 - sigma))
    hidden = (activated * pre_up).astype(jnp.bfloat16)
    all_hidden = lax.all_gather(hidden, "replica", axis=2, tiled=True).reshape(slot_count, -1)
    down_full = w_down.reshape(-1, slice_width)
    expert_out = jnp.dot(all_hidden, down_full, preferred_element_type=jnp.float32).astype(
        jnp.bfloat16
    )
    returned = lax.all_to_all(
        expert_out.reshape(experts_axis, capacity, slice_width),
        "expert",
        split_axis=0,
        concat_axis=0,
        tiled=True,
    ).reshape(slot_count, slice_width)
    picked = returned[target].astype(jnp.float32).reshape(tok_rows, top_count, slice_width)
    moe_out = jnp.sum(picked * gate_values[:, :, None], axis=1).astype(jnp.bfloat16)
    down_local = lax.dot_general(
        all_hidden, grads_part, (((0,), (0,)), ((), ())), preferred_element_type=jnp.float32
    )
    partial_value = lax.dot_general(
        grads_part, down_full, contract, preferred_element_type=jnp.float32
    )
    hidden_grad = lax.psum_scatter(
        partial_value.reshape(slot_count, 2, -1), "replica", scatter_dimension=2, tiled=True
    )
    gate_act = (hidden_grad * pre_up * slope_term).astype(jnp.bfloat16)
    up_act = (hidden_grad * activated).astype(jnp.bfloat16)
    gate_local = jnp.einsum("sd,shq->hqd", full_rows, gate_act, preferred_element_type=jnp.float32)
    up_local = jnp.einsum("sd,shq->hqd", full_rows, up_act, preferred_element_type=jnp.float32)
    all_gate_act, all_up_act = (
        lax.all_gather(gate_act, "replica", axis=2, tiled=True),
        lax.all_gather(up_act, "replica", axis=2, tiled=True),
    )
    rows_gate, rows_up = (
        lax.all_to_all(w_gate, "replica", split_axis=2, concat_axis=1, tiled=True),
        lax.all_to_all(w_up, "replica", split_axis=2, concat_axis=1, tiled=True),
    )
    input_rows = jnp.einsum(
        "shf,hfd->sd", all_gate_act, rows_gate, preferred_element_type=jnp.float32
    )
    input_rows = input_rows + jnp.einsum(
        "shf,hfd->sd", all_up_act, rows_up, preferred_element_type=jnp.float32
    )
    grads_back = lax.all_to_all(
        input_rows.astype(jnp.bfloat16).reshape(experts_axis, capacity, slice_width),
        "expert",
        split_axis=0,
        concat_axis=0,
        tiled=True,
    ).reshape(slot_count, slice_width)
    token_grad = jnp.sum(
        grads_back[target].astype(jnp.float32).reshape(tok_rows, top_count, slice_width), axis=1
    ).astype(jnp.bfloat16)
    keep_gate, give_gate = pick_half(parity_bit, gate_local, 0)
    keep_up, give_up = pick_half(parity_bit, up_local, 0)
    keep_down, give_down = pick_half(parity_bit, down_local.reshape(2, -1, slice_width), 0)
    received = (
        partner_2(give_gate.astype(jnp.bfloat16), "expert", 0).astype(give_gate.dtype),
        partner_2(give_up.astype(jnp.bfloat16), "expert", 0).astype(give_up.dtype),
        partner_2(give_down.astype(jnp.bfloat16), "expert", 0).astype(give_down.dtype),
    )
    gate_grad = (keep_gate + received[0]).astype(jnp.bfloat16)[None]
    up_grad = (keep_up + received[1]).astype(jnp.bfloat16)[None]
    down_grad = (keep_down + received[2]).astype(jnp.bfloat16)[None]
    return (moe_out, token_grad, gate_grad, up_grad, down_grad)


def dot(left, right, dims):
    return lax.dot_general(left, right, (dims, ((), ())), preferred_element_type=F32)


def gate_column(place, tables):
    table = jnp.concatenate([ref[...] for ref in tables], axis=0).astype(F32)
    lane = lax.broadcasted_iota(jnp.int32, table.shape, 1)
    count = place[3]
    mine = (lane == place[2]) | (lane == place[2] + count) | (lane == place[2] + 2 * count)
    return jnp.sum(jnp.where(mine, table, 0.0), axis=1, keepdims=True)


def columns(index, width):
    return pl.ds(pl.multiple_of(index * width, width), width)


def cotangent_kernel(place, og00, og01, og10, og11, down, keep, give):
    width, units = og00.shape[1], keep.shape[1]
    total = [None, None]
    for c_rel, parts in enumerate(((og00, og01), (og10, og11))):
        rows = jnp.concatenate([part[...] for part in parts], axis=0)
        for r_rel in range(2):
            block = down[columns(place[0] ^ r_rel, units), columns(place[1] ^ c_rel, width)]
            term = dot(rows, block, ((1,), (1,)))
            total[r_rel] = term if total[r_rel] is None else total[r_rel] + term
    keep[...] = total[0]
    give[...] = total[1].astype(give.dtype)


def hidden_kernel(place, x000, x001, x010, x011, x100, x101, x110, x111, t0, t1, gate, up,
                  hidden, act, slope):
    width = x000.shape[1]
    a = b = None
    for r_rel, c_rel, parts in ((0, 0, (x000, x001)), (0, 1, (x010, x011)),
                                (1, 0, (x100, x101)), (1, 1, (x110, x111))):
        rows = jnp.concatenate([part[...] for part in parts], axis=0)
        where = columns((place[0] ^ r_rel) * 2 + (place[1] ^ c_rel), width)
        term_a = dot(rows, gate[:, where], ((1,), (1,)))
        term_b = dot(rows, up[:, where], ((1,), (1,)))
        a = term_a if a is None else a + term_a
        b = term_b if b is None else b + term_b
    weight = gate_column(place, (t0, t1))
    sigma = jax.nn.sigmoid(a)
    silu = a * sigma
    hidden[...] = (weight * (silu * b)).astype(hidden.dtype)
    act[...] = weight * silu
    slope[...] = weight * (b * (sigma * (1.0 + a * (1.0 - sigma))))


def input_kernel(place, own, other, act, slope, gate, up, da_out, db_out, keep, give):
    width = keep.shape[2]
    dh = own[...] + other[...].astype(F32)
    da = (dh * slope[...]).astype(BF16)
    db = (dh * act[...]).astype(BF16)
    da_out[...] = da
    db_out[...] = db
    for r_rel in range(2):
        for c_rel in range(2):
            where = columns((place[0] ^ r_rel) * 2 + (place[1] ^ c_rel), width)
            block = dot(da, gate[:, where], ((1,), (0,))) + dot(db, up[:, where], ((1,), (0,)))
            if c_rel == 0:
                keep[r_rel] = block
            else:
                give[r_rel] = block.astype(give.dtype)


def output_kernel(place, own, other, down, keep, give):
    width, units = keep.shape[1], own.shape[1]
    for c_rel in range(2):
        where = columns(place[1] ^ c_rel, width)
        block = dot(own[...], down[columns(place[0], units), where], ((1,), (0,)))
        block = block + dot(other[...], down[columns(place[0] ^ 1, units), where], ((1,), (0,)))
        if c_rel == 0:
            keep[...] = block
        else:
            give[...] = block.astype(give.dtype)


def down_grad_kernel(place, own, other, og00, og01, og10, og11, down_grad):
    width, units = og00.shape[1], own.shape[1]
    for c_rel, parts in enumerate(((og00, og01), (og10, og11))):
        rows = jnp.concatenate([part[...] for part in parts], axis=0)
        for r_rel, hidden in ((0, own), (1, other)):
            block = dot(hidden[...], rows, ((0,), (0,)))
            down_grad[columns(place[0] ^ r_rel, units), columns(place[1] ^ c_rel, width)] = (
                block.astype(down_grad.dtype)
            )


def weight_grad_kernel(place, da, db, x000, x001, x010, x011, x100, x101, x110, x111,
                       gate_grad, up_grad):
    width = x000.shape[1]
    for r_rel, c_rel, parts in ((0, 0, (x000, x001)), (0, 1, (x010, x011)),
                                (1, 0, (x100, x101)), (1, 1, (x110, x111))):
        rows = jnp.concatenate([part[...] for part in parts], axis=0)
        where = columns((place[0] ^ r_rel) * 2 + (place[1] ^ c_rel), width)
        gate_grad[:, where] = dot(da[...], rows, ((0,), (0,))).astype(gate_grad.dtype)
        up_grad[:, where] = dot(db[...], rows, ((0,), (0,))).astype(up_grad.dtype)


def call(kernel, place, operands, outs, flops):
    moved = sum(x.size * x.dtype.itemsize for x in (*operands, *outs))
    vmem = pl.BlockSpec(memory_space=pltpu.VMEM)
    return pl.pallas_call(
        kernel,
        out_shape=list(outs),
        in_specs=[pl.BlockSpec(memory_space=pltpu.SMEM)] + [vmem] * len(operands),
        out_specs=[vmem] * len(outs),
        compiler_params=pltpu.CompilerParams(vmem_limit_bytes=24 << 20),
        cost_estimate=pl.CostEstimate(flops=flops, bytes_accessed=moved, transcendentals=0),
    )(place, *operands)


def struct(shape, dtype):
    return jax.ShapeDtypeStruct(shape, dtype)


def swap(value, expert_bits, replica_bit=0):
    count, replicas = lax.axis_size("expert"), lax.axis_size("replica")
    if not replica_bit:
        return lax.ppermute(value, "expert", [(i, i ^ expert_bits) for i in range(count)])
    if not expert_bits:
        return lax.ppermute(value, "replica", [(i, i ^ replica_bit) for i in range(replicas)])
    flip = expert_bits * replicas + replica_bit
    return lax.ppermute(
        value, ("expert", "replica"), [(i, i ^ flip) for i in range(count * replicas)]
    )


def dense_device(tokens, expert_ids, gate_values, gate_weight, up_weight, down_weight, out_grad):
    devices = lax.axis_size("expert")
    experts, far = devices // 2, devices // 4
    tok_rows, slice_width = tokens.shape
    half = slice_width // 2
    me = lax.axis_index("expert")
    core, replica = me % 2, lax.axis_index("replica")
    place = jnp.stack([replica, core, me // 2, jnp.int32(experts)]).astype(jnp.int32)
    gate, up, down = gate_weight[0], up_weight[0], down_weight[0]
    units, model_width = gate.shape

    def order(own, peer, axis):
        return jnp.where(
            core == 0,
            jnp.concatenate([own, peer], axis=axis),
            jnp.concatenate([peer, own], axis=axis),
        )

    routed = expert_ids[:, :, None] == jnp.arange(experts, dtype=jnp.int32)
    table = jnp.sum(jnp.where(routed, gate_values[:, :, None], 0.0), axis=1)
    parts = []
    for _ in range(3):
        part = lax.reduce_precision(table, 8, 7)
        parts.append(part.astype(BF16))
        table = table - part
    coded = jnp.concatenate(parts, axis=1)
    coded = jnp.pad(coded, ((0, 0), (0, -coded.shape[1] % LANES)))

    low = jnp.concatenate([tokens[:, :half], out_grad[:, :half], coded], axis=1)
    high = jnp.concatenate([tokens[:, half:], out_grad[:, half:], coded], axis=1)
    mine, theirs = jnp.where(core == 0, low, high), jnp.where(core == 0, high, low)
    block = order(mine, swap(theirs, 1), 0)
    blocks = [block] + [swap(block, 4 * step) for step in range(1, far)]
    x_here = jnp.concatenate([part[:, :half] for part in blocks], axis=0)
    og_here = jnp.concatenate([part[:, half : 2 * half] for part in blocks], axis=0)
    t_here = jnp.concatenate([part[:, 2 * half :] for part in blocks], axis=0)
    og_side = swap(og_here, 2)
    t_side = swap(t_here, 2)
    x_side, x_up, x_cross = swap(x_here, 2), swap(x_here, 0, 1), swap(x_here, 2, 1)
    og = [og_here, og_side, swap(og_here, 1), swap(og_side, 1)]
    x = [x_here, x_side, swap(x_here, 1), swap(x_side, 1),
         x_up, x_cross, swap(x_up, 1), swap(x_cross, 1)]
    side_rows = x_here.shape[0]
    all_rows = 2 * side_rows
    work = 2 * all_rows * units

    d_own, d_give = call(
        cotangent_kernel, place, (*og, down),
        (struct((all_rows, units), F32), struct((all_rows, units), BF16)),
        work * 2 * slice_width,
    )
    d_got = swap(d_give, 0, 1)
    hidden, act, slope = call(
        hidden_kernel, place, (*x, t_here, t_side, gate, up),
        (struct((all_rows, units), BF16), struct((all_rows, units), F32),
         struct((all_rows, units), F32)),
        work * 2 * model_width,
    )
    hidden_got = swap(hidden, 0, 1)
    da, db, dx_keep, dx_give = call(
        input_kernel, place, (d_own, d_got, act, slope, gate, up),
        (struct((all_rows, units), BF16), struct((all_rows, units), BF16),
         struct((2, all_rows, half), F32), struct((2, all_rows, half), BF16)),
        work * 2 * model_width,
    )
    y_keep, y_give = call(
        output_kernel, place, (hidden, hidden_got, down),
        (struct((all_rows, half), F32), struct((all_rows, half), BF16)),
        work * 2 * slice_width,
    )
    (down_grad,) = call(
        down_grad_kernel, place, (hidden, hidden_got, *og),
        (struct(down.shape, BF16),), work * 2 * slice_width,
    )
    gate_grad, up_grad = call(
        weight_grad_kernel, place, (da, db, *x),
        (struct(gate.shape, BF16), struct(up.shape, BF16)), work * 2 * model_width,
    )

    dx = dx_keep + swap(dx_give, 1).astype(F32)
    y = y_keep + swap(y_give, 1).astype(F32)
    dx_side = swap(dx[0, side_rows:].astype(BF16), 2)
    dx_up = swap(dx[1, :side_rows].astype(BF16), 0, 1)
    dx_cross = swap(dx[1, side_rows:].astype(BF16), 2, 1)
    y_side = swap(y[side_rows:].astype(BF16), 2)
    dx_sum = (dx[0, :side_rows] + dx_side.astype(F32)) + (dx_up.astype(F32) + dx_cross.astype(F32))
    y_sum = y[:side_rows] + y_side.astype(F32)
    both = jnp.concatenate([y_sum, dx_sum], axis=1)
    pair = 2 * tok_rows
    total = both[:pair]
    for step in range(1, far):
        part = both[step * pair : (step + 1) * pair].astype(BF16)
        total = total + swap(part, 4 * step).astype(F32)
    total = total.astype(BF16)
    first, second = total[:tok_rows], total[tok_rows:]
    kept = jnp.where(core == 0, first, second)
    got = swap(jnp.where(core == 0, second, first), 1)
    moe_out = order(kept[:, :half], got[:, :half], 1)
    token_grad = order(kept[:, half:], got[:, half:], 1)
    return moe_out, token_grad, gate_grad[None], up_grad[None], down_grad[None]


def per_device(tokens, expert_ids, gate_values, gate_weight, up_weight, down_weight, out_grad):
    devices, replicas = lax.axis_size("expert"), lax.axis_size("replica")
    every_expert = expert_ids.shape[1] == devices // 2
    power = devices & (devices - 1) == 0 and devices >= 4
    aligned = tokens.shape[1] % (2 * LANES) == 0 and gate_weight.shape[1] % LANES == 0
    use_dense = every_expert and power and replicas == 2 and aligned
    body = dense_device if use_dense else routed_device
    return body(
        tokens, expert_ids, gate_values, gate_weight, up_weight, down_weight, out_grad
    )


def solution(mesh):
    placed = (
        P("expert", "replica"),
        P("expert", None),
        P("expert", None),
        P("expert", "replica", None),
        P("expert", "replica", None),
        P("expert", None, "replica"),
        P("expert", "replica"),
    )
    return jax.shard_map(
        per_device,
        mesh=mesh,
        in_specs=placed,
        out_specs=(
            P("expert", "replica"),
            P("expert", "replica"),
            P("expert", "replica", None),
            P("expert", "replica", None),
            P("expert", None, "replica"),
        ),
        check_vma=False,
    )
```

```python
import jax
import jax.numpy as jnp
from jax import lax
from jax.experimental import pallas as pl
from jax.experimental.pallas import tpu as pltpu
from jax.sharding import PartitionSpec as P


BF16, F32 = jnp.bfloat16, jnp.float32
LANES = 128


def partner_2(block, axis, distance):
    count = lax.axis_size(axis)
    route = []
    for low in range(count):
        high = low | 1 << distance
        if high != low and high < count:
            route += [(low, high), (high, low)]
    return lax.ppermute(block, axis, route)


def pair_join(parity_bit, own_part, peer_part, stack_axis):
    first_part = jnp.where(parity_bit == 0, own_part, peer_part)
    second_part = jnp.where(parity_bit == 0, peer_part, own_part)
    return jnp.stack([first_part, second_part], axis=stack_axis)


def pick_half(parity_bit, stacked, stack_axis):
    lower = jnp.take(stacked, 0, axis=stack_axis)
    higher = jnp.take(stacked, 1, axis=stack_axis)
    return (jnp.where(parity_bit == 0, lower, higher), jnp.where(parity_bit == 0, higher, lower))


def routed_device(tokens, expert_ids, gate_values, gate_weight, up_weight, down_weight, out_grad):
    experts_axis = lax.axis_size("expert")
    tok_rows, slice_width = tokens.shape
    top_count = expert_ids.shape[1]
    expert_count = experts_axis // 2
    most_rows = min(tok_rows, 4 * tok_rows * top_count // (3 * expert_count))
    capacity = (most_rows + 1) // 2
    pair_count = tok_rows * top_count
    slot_count = experts_axis * capacity
    flat_ids = expert_ids.reshape(pair_count)
    onehot = (flat_ids[:, None] == jnp.arange(expert_count, dtype=jnp.int32)[None, :]).astype(
        jnp.int32
    )
    rank_in = jnp.sum((jnp.cumsum(onehot, axis=0) - onehot) * onehot, axis=1)
    upper_copy = (rank_in >= capacity).astype(jnp.int32)
    target = (2 * flat_ids + upper_copy) * capacity + rank_in - upper_copy * capacity
    slot_match = target[None, :] == jnp.arange(slot_count, dtype=jnp.int32)[:, None]
    filled = jnp.any(slot_match, axis=1)
    source_pair = jnp.sum(
        jnp.where(slot_match, jnp.arange(pair_count, dtype=jnp.int32)[None, :], 0), axis=1
    )
    source_token = source_pair // top_count
    flat_gates = gate_values.reshape(pair_count)
    send_rows = jnp.where(filled[:, None], tokens[source_token], jnp.zeros((), tokens.dtype))
    scaled = flat_gates[source_pair][:, None] * out_grad[source_token].astype(jnp.float32)
    send_grads = jnp.where(filled[:, None], scaled, 0.0).astype(jnp.bfloat16)
    got_rows, got_grads = (
        lax.all_to_all(
            send_rows.reshape(experts_axis, capacity, slice_width),
            "expert",
            split_axis=0,
            concat_axis=0,
            tiled=True,
        ),
        lax.all_to_all(
            send_grads.reshape(experts_axis, capacity, slice_width),
            "expert",
            split_axis=0,
            concat_axis=0,
            tiled=True,
        ),
    )
    rows_part = got_rows.reshape(slot_count, slice_width)
    grads_part = got_grads.reshape(slot_count, slice_width)
    parity_bit = lax.axis_index("expert") % 2
    own_pieces = (gate_weight[0], up_weight[0], down_weight[0])
    partner = partner_2((own_pieces[0], own_pieces[1], own_pieces[2]), "expert", 0)
    w_gate = pair_join(parity_bit, own_pieces[0], partner[0], 0)
    w_up = pair_join(parity_bit, own_pieces[1], partner[1], 0)
    w_down = pair_join(parity_bit, own_pieces[2], partner[2], 0)
    _, quarter, model_width = w_gate.shape
    full_rows = lax.all_gather(rows_part, "replica", axis=1, tiled=True)
    contract = (((1,), (1,)), ((), ()))
    pre_gate = lax.dot_general(
        full_rows,
        w_gate.reshape(2 * quarter, model_width),
        contract,
        preferred_element_type=jnp.float32,
    ).reshape(slot_count, 2, quarter)
    pre_up = lax.dot_general(
        full_rows,
        w_up.reshape(2 * quarter, model_width),
        contract,
        preferred_element_type=jnp.float32,
    ).reshape(slot_count, 2, quarter)
    sigma = jax.nn.sigmoid(pre_gate)
    activated = pre_gate * sigma
    slope_term = sigma * (1.0 + pre_gate * (1.0 - sigma))
    hidden = (activated * pre_up).astype(jnp.bfloat16)
    all_hidden = lax.all_gather(hidden, "replica", axis=2, tiled=True).reshape(slot_count, -1)
    down_full = w_down.reshape(-1, slice_width)
    expert_out = jnp.dot(all_hidden, down_full, preferred_element_type=jnp.float32).astype(
        jnp.bfloat16
    )
    returned = lax.all_to_all(
        expert_out.reshape(experts_axis, capacity, slice_width),
        "expert",
        split_axis=0,
        concat_axis=0,
        tiled=True,
    ).reshape(slot_count, slice_width)
    picked = returned[target].astype(jnp.float32).reshape(tok_rows, top_count, slice_width)
    moe_out = jnp.sum(picked * gate_values[:, :, None], axis=1).astype(jnp.bfloat16)
    down_local = lax.dot_general(
        all_hidden, grads_part, (((0,), (0,)), ((), ())), preferred_element_type=jnp.float32
    )
    partial_value = lax.dot_general(
        grads_part, down_full, contract, preferred_element_type=jnp.float32
    )
    hidden_grad = lax.psum_scatter(
        partial_value.reshape(slot_count, 2, -1), "replica", scatter_dimension=2, tiled=True
    )
    gate_act = (hidden_grad * pre_up * slope_term).astype(jnp.bfloat16)
    up_act = (hidden_grad * activated).astype(jnp.bfloat16)
    gate_local = jnp.einsum("sd,shq->hqd", full_rows, gate_act, preferred_element_type=jnp.float32)
    up_local = jnp.einsum("sd,shq->hqd", full_rows, up_act, preferred_element_type=jnp.float32)
    all_gate_act, all_up_act = (
        lax.all_gather(gate_act, "replica", axis=2, tiled=True),
        lax.all_gather(up_act, "replica", axis=2, tiled=True),
    )
    rows_gate, rows_up = (
        lax.all_to_all(w_gate, "replica", split_axis=2, concat_axis=1, tiled=True),
        lax.all_to_all(w_up, "replica", split_axis=2, concat_axis=1, tiled=True),
    )
    input_rows = jnp.einsum(
        "shf,hfd->sd", all_gate_act, rows_gate, preferred_element_type=jnp.float32
    )
    input_rows = input_rows + jnp.einsum(
        "shf,hfd->sd", all_up_act, rows_up, preferred_element_type=jnp.float32
    )
    grads_back = lax.all_to_all(
        input_rows.astype(jnp.bfloat16).reshape(experts_axis, capacity, slice_width),
        "expert",
        split_axis=0,
        concat_axis=0,
        tiled=True,
    ).reshape(slot_count, slice_width)
    token_grad = jnp.sum(
        grads_back[target].astype(jnp.float32).reshape(tok_rows, top_count, slice_width), axis=1
    ).astype(jnp.bfloat16)
    keep_gate, give_gate = pick_half(parity_bit, gate_local, 0)
    keep_up, give_up = pick_half(parity_bit, up_local, 0)
    keep_down, give_down = pick_half(parity_bit, down_local.reshape(2, -1, slice_width), 0)
    received = (
        partner_2(give_gate.astype(jnp.bfloat16), "expert", 0).astype(give_gate.dtype),
        partner_2(give_up.astype(jnp.bfloat16), "expert", 0).astype(give_up.dtype),
        partner_2(give_down.astype(jnp.bfloat16), "expert", 0).astype(give_down.dtype),
    )
    gate_grad = (keep_gate + received[0]).astype(jnp.bfloat16)[None]
    up_grad = (keep_up + received[1]).astype(jnp.bfloat16)[None]
    down_grad = (keep_down + received[2]).astype(jnp.bfloat16)[None]
    return (moe_out, token_grad, gate_grad, up_grad, down_grad)


def dot(left, right, dims):
    return lax.dot_general(left, right, (dims, ((), ())), preferred_element_type=F32)


def gate_column(place, tables):
    table = jnp.concatenate([ref[:, -LANES:] for ref in tables], axis=0).astype(F32)
    lane = lax.broadcasted_iota(jnp.int32, table.shape, 1)
    count = place[3]
    mine = (lane == place[2]) | (lane == place[2] + count) | (lane == place[2] + 2 * count)
    return jnp.sum(jnp.where(mine, table, 0.0), axis=1, keepdims=True)


def columns(index, width):
    return pl.ds(pl.multiple_of(index * width, width), width)


def load_kernel(place, gate_hbm, up_hbm, down_hbm, gate, up, down, sems):
    copies = [pltpu.make_async_copy(source, target, sems.at[n])
              for n, (source, target) in enumerate(
                  ((down_hbm, down), (gate_hbm, gate), (up_hbm, up)))]
    for copy in copies:
        copy.start()
    for copy in copies:
        copy.wait()


def cotangent_kernel(place, og00, og01, og10, og11, down, keep, give):
    width, units = og10.shape[1], keep.shape[1]
    total = [None, None]
    for c_rel, parts in enumerate(((og00, og01), (og10, og11))):
        rows = jnp.concatenate([part[:, :width] for part in parts], axis=0)
        for r_rel in range(2):
            block = down[columns(place[0] ^ r_rel, units), columns(place[1] ^ c_rel, width)]
            term = dot(rows, block, ((1,), (1,)))
            total[r_rel] = term if total[r_rel] is None else total[r_rel] + term
    keep[...] = total[0]
    give[...] = total[1].astype(give.dtype)


def hidden_kernel(place, x000, x001, x010, x011, x100, x101, x110, x111, t0, t1, gate, up,
                  hidden, act, slope):
    width = x000.shape[1]
    a = b = None
    for r_rel, c_rel, parts in ((0, 0, (x000, x001)), (0, 1, (x010, x011)),
                                (1, 0, (x100, x101)), (1, 1, (x110, x111))):
        rows = jnp.concatenate([part[...] for part in parts], axis=0)
        where = columns((place[0] ^ r_rel) * 2 + (place[1] ^ c_rel), width)
        term_a = dot(rows, gate[:, where], ((1,), (1,)))
        term_b = dot(rows, up[:, where], ((1,), (1,)))
        a = term_a if a is None else a + term_a
        b = term_b if b is None else b + term_b
    weight = gate_column(place, (t0, t1))
    sigma = jax.nn.sigmoid(a)
    silu = a * sigma
    hidden[...] = (weight * (silu * b)).astype(hidden.dtype)
    act[...] = weight * silu
    slope[...] = weight * (b * (sigma * (1.0 + a * (1.0 - sigma))))


def input_kernel(place, own, other, act, slope, gate, up, da_out, db_out, keep, give):
    width = keep.shape[2]
    dh = own[...] + other[...].astype(F32)
    da = (dh * slope[...]).astype(BF16)
    db = (dh * act[...]).astype(BF16)
    da_out[...] = da
    db_out[...] = db
    for r_rel in range(2):
        for c_rel in range(2):
            where = columns((place[0] ^ r_rel) * 2 + (place[1] ^ c_rel), width)
            block = dot(da, gate[:, where], ((1,), (0,))) + dot(db, up[:, where], ((1,), (0,)))
            if c_rel == 0:
                keep[r_rel] = block
            else:
                give[r_rel] = block.astype(give.dtype)


def output_kernel(place, own, other, down, keep, give):
    width, units = keep.shape[1], own.shape[1]
    for c_rel in range(2):
        where = columns(place[1] ^ c_rel, width)
        block = dot(own[...], down[columns(place[0], units), where], ((1,), (0,)))
        block = block + dot(other[...], down[columns(place[0] ^ 1, units), where], ((1,), (0,)))
        if c_rel == 0:
            keep[...] = block
        else:
            give[...] = block.astype(give.dtype)


def down_grad_kernel(place, own, other, og00, og01, og10, og11, down_grad):
    width, units = og10.shape[1], own.shape[1]
    for c_rel, parts in enumerate(((og00, og01), (og10, og11))):
        rows = jnp.concatenate([part[:, :width] for part in parts], axis=0)
        for r_rel, hidden in ((0, own), (1, other)):
            block = dot(hidden[...], rows, ((0,), (0,)))
            down_grad[columns(place[0] ^ r_rel, units), columns(place[1] ^ c_rel, width)] = (
                block.astype(down_grad.dtype)
            )


def weight_grad_kernel(place, da, db, x000, x001, x010, x011, x100, x101, x110, x111,
                       gate_grad, up_grad):
    width = x000.shape[1]
    for r_rel, c_rel, parts in ((0, 0, (x000, x001)), (0, 1, (x010, x011)),
                                (1, 0, (x100, x101)), (1, 1, (x110, x111))):
        rows = jnp.concatenate([part[...] for part in parts], axis=0)
        where = columns((place[0] ^ r_rel) * 2 + (place[1] ^ c_rel), width)
        gate_grad[:, where] = dot(da[...], rows, ((0,), (0,))).astype(gate_grad.dtype)
        up_grad[:, where] = dot(db[...], rows, ((0,), (0,))).astype(up_grad.dtype)


def call(kernel, place, operands, outs, flops, in_hbm=(), scratch=(), limit=24 << 20):
    moved = sum(x.size * x.dtype.itemsize for x in (*operands, *outs))
    vmem = pl.BlockSpec(memory_space=pltpu.VMEM)
    hbm = pl.BlockSpec(memory_space=pltpu.HBM)
    return pl.pallas_call(
        kernel,
        out_shape=list(outs),
        in_specs=[pl.BlockSpec(memory_space=pltpu.SMEM)]
        + [hbm if n in in_hbm else vmem for n in range(len(operands))],
        out_specs=[vmem] * len(outs),
        scratch_shapes=list(scratch),
        compiler_params=pltpu.CompilerParams(vmem_limit_bytes=limit),
        cost_estimate=pl.CostEstimate(flops=flops, bytes_accessed=moved, transcendentals=0),
    )(place, *operands)


def struct(shape, dtype):
    return jax.ShapeDtypeStruct(shape, dtype)


def swap(value, expert_bits, replica_bit=0):
    count, replicas = lax.axis_size("expert"), lax.axis_size("replica")
    flip = expert_bits * replicas + replica_bit
    if not replica_bit:
        return lax.ppermute(value, "expert", [(i, i ^ expert_bits) for i in range(count)])
    if not expert_bits:
        return lax.ppermute(value, "replica", [(i, i ^ flip) for i in range(replicas)])
    return lax.ppermute(
        value, ("expert", "replica"), [(i, i ^ flip) for i in range(count * replicas)]
    )


def dense_device(tokens, expert_ids, gate_values, gate_weight, up_weight, down_weight, out_grad):
    devices = lax.axis_size("expert")
    experts, far = devices // 2, devices // 4
    tok_rows, slice_width = tokens.shape
    half = slice_width // 2
    me = lax.axis_index("expert")
    core, replica = me % 2, lax.axis_index("replica")
    place = jnp.stack([replica, core, me // 2, jnp.int32(experts)]).astype(jnp.int32)
    gate, up, down = gate_weight[0], up_weight[0], down_weight[0]
    units, model_width = gate.shape

    def order(own, peer, axis):
        return jnp.where(
            core == 0,
            jnp.concatenate([own, peer], axis=axis),
            jnp.concatenate([peer, own], axis=axis),
        )

    routed = expert_ids[:, :, None] == jnp.arange(experts, dtype=jnp.int32)
    table = jnp.sum(jnp.where(routed, gate_values[:, :, None], 0.0), axis=1)
    parts = []
    for _ in range(3):
        part = lax.reduce_precision(table, 8, 7)
        parts.append(part.astype(BF16))
        table = table - part
    coded = jnp.concatenate(parts, axis=1)
    coded = jnp.pad(coded, ((0, 0), (0, -coded.shape[1] % LANES)))
    own = lax.optimization_barrier(jnp.concatenate([tokens, out_grad], axis=1))
    low = jnp.concatenate([own[:, :half], own[:, 2 * half : 3 * half], coded], axis=1)
    high = jnp.concatenate([own[:, half : 2 * half], own[:, 3 * half :], coded], axis=1)
    mine, theirs = jnp.where(core == 0, low, high), jnp.where(core == 0, high, low)
    gate, up, down = call(
        load_kernel, place, (gate, up, down),
        [struct(w.shape, w.dtype) for w in (gate, up, down)], 0, in_hbm=(0, 1, 2),         scratch=[pltpu.SemaphoreType.DMA((3,))],
    )
    block = order(mine, swap(theirs, 1), 0)
    got = {step: swap(block, 4 * step) for step in reversed(range(1, far))}
    blocks = [block] + [got[step] for step in range(1, far)]
    og_here = jnp.concatenate([part[:, half:] for part in blocks], axis=0)
    x_here = jnp.concatenate([part[:, :half] for part in blocks], axis=0)
    og_side = swap(og_here, 2)
    x_side = swap(x_here, 2)
    x_cross = swap(x_here, 2, 1)
    x_up = swap(x_here, 0, 1)
    og = [og_here, og_side,
          swap(og_here[:, :half], 1), swap(og_side[:, :half], 1)]
    x = [x_here, x_side, swap(x_here, 1), swap(x_side, 1),
         x_up, x_cross, swap(x_up, 1), swap(x_cross, 1)]
    side_rows = x_here.shape[0]
    all_rows = 2 * side_rows
    work = 2 * all_rows * units

    d_own, d_give = call(
        cotangent_kernel, place, (*og, down),
        (struct((all_rows, units), F32), struct((all_rows, units), BF16)),
        work * 2 * slice_width,
    )
    d_got = swap(d_give, 0, 1)
    hidden, act, slope = call(
        hidden_kernel, place, (*x, og_here, og_side, gate, up),
        (struct((all_rows, units), BF16), struct((all_rows, units), F32),
         struct((all_rows, units), F32)),
        work * 2 * model_width,
    )
    hidden_got = swap(hidden, 0, 1)
    da, db, dx_keep, dx_give = call(
        input_kernel, place, (d_own, d_got, act, slope, gate, up),
        (struct((all_rows, units), BF16), struct((all_rows, units), BF16),
         struct((2, all_rows, half), F32), struct((2, all_rows, half), BF16)),
        work * 2 * model_width,
    )
    dx = dx_keep + swap(dx_give, 1).astype(F32)
    dx_cross = swap(dx[1, side_rows:].astype(BF16), 2, 1)
    dx_side = swap(dx[0, side_rows:].astype(BF16), 2)
    dx_up = swap(dx[1, :side_rows].astype(BF16), 0, 1)

    y_keep, y_give = call(
        output_kernel, place, (hidden, hidden_got, down),
        (struct((all_rows, half), F32), struct((all_rows, half), BF16)),
        work * 2 * slice_width,
    )
    y = y_keep + swap(y_give, 1).astype(F32)
    y_side = swap(y[side_rows:].astype(BF16), 2)
    (down_grad,) = call(
        down_grad_kernel, place, (hidden, hidden_got, *og),
        (struct(down.shape, BF16),), work * 2 * slice_width,
    )
    gate_grad, up_grad = call(
        weight_grad_kernel, place, (da, db, *x),
        (struct(gate.shape, BF16), struct(up.shape, BF16)), work * 2 * model_width,
    )

    dx_sum = (dx[0, :side_rows] + dx_side.astype(F32)) + (dx_up.astype(F32) + dx_cross.astype(F32))
    y_sum = y[:side_rows] + y_side.astype(F32)
    both = jnp.concatenate([y_sum, dx_sum], axis=1)
    pair = 2 * tok_rows
    total = both[:pair]
    for step in reversed(range(1, far)):
        part = both[step * pair : (step + 1) * pair].astype(BF16)
        total = total + swap(part, 4 * step).astype(F32)
    total = total.astype(BF16)
    first, second = total[:tok_rows], total[tok_rows:]
    kept = jnp.where(core == 0, first, second)
    got = swap(jnp.where(core == 0, second, first), 1)
    moe_out = order(kept[:, :half], got[:, :half], 1)
    token_grad = order(kept[:, half:], got[:, half:], 1)
    return moe_out, token_grad, gate_grad[None], up_grad[None], down_grad[None]


def per_device(tokens, expert_ids, gate_values, gate_weight, up_weight, down_weight, out_grad):
    args = (tokens, expert_ids, gate_values, gate_weight, up_weight, down_weight, out_grad)
    devices, replicas = lax.axis_size("expert"), lax.axis_size("replica")
    every_expert = expert_ids.shape[1] == devices // 2
    power = devices & (devices - 1) == 0 and devices >= 4 and 3 * (devices // 2) <= LANES
    aligned = tokens.shape[1] % (2 * LANES) == 0 and gate_weight.shape[1] % LANES == 0
    if every_expert and power and replicas == 2 and aligned:
        return dense_device(*args)
    return routed_device(*args)


def solution(mesh):
    placed = (
        P("expert", "replica"),
        P("expert", None),
        P("expert", None),
        P("expert", "replica", None),
        P("expert", "replica", None),
        P("expert", None, "replica"),
        P("expert", "replica"),
    )
    return jax.shard_map(
        per_device,
        mesh=mesh,
        in_specs=placed,
        out_specs=(
            P("expert", "replica"),
            P("expert", "replica"),
            P("expert", "replica", None),
            P("expert", "replica", None),
            P("expert", None, "replica"),
        ),
        check_vma=False,
    )
```

```python
import jax
import jax.numpy as jnp
from jax import lax
from jax.experimental import pallas as pl
from jax.experimental.pallas import tpu as pltpu
from jax.sharding import PartitionSpec as P


BF16, F32 = jnp.bfloat16, jnp.float32
LANES = 128


def partner_2(block, axis, distance):
    count = lax.axis_size(axis)
    route = []
    for low in range(count):
        high = low | 1 << distance
        if high != low and high < count:
            route += [(low, high), (high, low)]
    return lax.ppermute(block, axis, route)


def pair_join(parity_bit, own_part, peer_part, stack_axis):
    first_part = jnp.where(parity_bit == 0, own_part, peer_part)
    second_part = jnp.where(parity_bit == 0, peer_part, own_part)
    return jnp.stack([first_part, second_part], axis=stack_axis)


def pick_half(parity_bit, stacked, stack_axis):
    lower = jnp.take(stacked, 0, axis=stack_axis)
    higher = jnp.take(stacked, 1, axis=stack_axis)
    return (jnp.where(parity_bit == 0, lower, higher), jnp.where(parity_bit == 0, higher, lower))


def routed_device(tokens, expert_ids, gate_values, gate_weight, up_weight, down_weight, out_grad):
    experts_axis = lax.axis_size("expert")
    tok_rows, slice_width = tokens.shape
    top_count = expert_ids.shape[1]
    expert_count = experts_axis // 2
    most_rows = min(tok_rows, 4 * tok_rows * top_count // (3 * expert_count))
    capacity = (most_rows + 1) // 2
    pair_count = tok_rows * top_count
    slot_count = experts_axis * capacity
    flat_ids = expert_ids.reshape(pair_count)
    onehot = (flat_ids[:, None] == jnp.arange(expert_count, dtype=jnp.int32)[None, :]).astype(
        jnp.int32
    )
    rank_in = jnp.sum((jnp.cumsum(onehot, axis=0) - onehot) * onehot, axis=1)
    upper_copy = (rank_in >= capacity).astype(jnp.int32)
    target = (2 * flat_ids + upper_copy) * capacity + rank_in - upper_copy * capacity
    slot_match = target[None, :] == jnp.arange(slot_count, dtype=jnp.int32)[:, None]
    filled = jnp.any(slot_match, axis=1)
    source_pair = jnp.sum(
        jnp.where(slot_match, jnp.arange(pair_count, dtype=jnp.int32)[None, :], 0), axis=1
    )
    source_token = source_pair // top_count
    flat_gates = gate_values.reshape(pair_count)
    send_rows = jnp.where(filled[:, None], tokens[source_token], jnp.zeros((), tokens.dtype))
    scaled = flat_gates[source_pair][:, None] * out_grad[source_token].astype(jnp.float32)
    send_grads = jnp.where(filled[:, None], scaled, 0.0).astype(jnp.bfloat16)
    got_rows, got_grads = (
        lax.all_to_all(
            send_rows.reshape(experts_axis, capacity, slice_width),
            "expert",
            split_axis=0,
            concat_axis=0,
            tiled=True,
        ),
        lax.all_to_all(
            send_grads.reshape(experts_axis, capacity, slice_width),
            "expert",
            split_axis=0,
            concat_axis=0,
            tiled=True,
        ),
    )
    rows_part = got_rows.reshape(slot_count, slice_width)
    grads_part = got_grads.reshape(slot_count, slice_width)
    parity_bit = lax.axis_index("expert") % 2
    own_pieces = (gate_weight[0], up_weight[0], down_weight[0])
    partner = partner_2((own_pieces[0], own_pieces[1], own_pieces[2]), "expert", 0)
    w_gate = pair_join(parity_bit, own_pieces[0], partner[0], 0)
    w_up = pair_join(parity_bit, own_pieces[1], partner[1], 0)
    w_down = pair_join(parity_bit, own_pieces[2], partner[2], 0)
    _, quarter, model_width = w_gate.shape
    full_rows = lax.all_gather(rows_part, "replica", axis=1, tiled=True)
    contract = (((1,), (1,)), ((), ()))
    pre_gate = lax.dot_general(
        full_rows,
        w_gate.reshape(2 * quarter, model_width),
        contract,
        preferred_element_type=jnp.float32,
    ).reshape(slot_count, 2, quarter)
    pre_up = lax.dot_general(
        full_rows,
        w_up.reshape(2 * quarter, model_width),
        contract,
        preferred_element_type=jnp.float32,
    ).reshape(slot_count, 2, quarter)
    sigma = jax.nn.sigmoid(pre_gate)
    activated = pre_gate * sigma
    slope_term = sigma * (1.0 + pre_gate * (1.0 - sigma))
    hidden = (activated * pre_up).astype(jnp.bfloat16)
    all_hidden = lax.all_gather(hidden, "replica", axis=2, tiled=True).reshape(slot_count, -1)
    down_full = w_down.reshape(-1, slice_width)
    expert_out = jnp.dot(all_hidden, down_full, preferred_element_type=jnp.float32).astype(
        jnp.bfloat16
    )
    returned = lax.all_to_all(
        expert_out.reshape(experts_axis, capacity, slice_width),
        "expert",
        split_axis=0,
        concat_axis=0,
        tiled=True,
    ).reshape(slot_count, slice_width)
    picked = returned[target].astype(jnp.float32).reshape(tok_rows, top_count, slice_width)
    moe_out = jnp.sum(picked * gate_values[:, :, None], axis=1).astype(jnp.bfloat16)
    down_local = lax.dot_general(
        all_hidden, grads_part, (((0,), (0,)), ((), ())), preferred_element_type=jnp.float32
    )
    partial_value = lax.dot_general(
        grads_part, down_full, contract, preferred_element_type=jnp.float32
    )
    hidden_grad = lax.psum_scatter(
        partial_value.reshape(slot_count, 2, -1), "replica", scatter_dimension=2, tiled=True
    )
    gate_act = (hidden_grad * pre_up * slope_term).astype(jnp.bfloat16)
    up_act = (hidden_grad * activated).astype(jnp.bfloat16)
    gate_local = jnp.einsum("sd,shq->hqd", full_rows, gate_act, preferred_element_type=jnp.float32)
    up_local = jnp.einsum("sd,shq->hqd", full_rows, up_act, preferred_element_type=jnp.float32)
    all_gate_act, all_up_act = (
        lax.all_gather(gate_act, "replica", axis=2, tiled=True),
        lax.all_gather(up_act, "replica", axis=2, tiled=True),
    )
    rows_gate, rows_up = (
        lax.all_to_all(w_gate, "replica", split_axis=2, concat_axis=1, tiled=True),
        lax.all_to_all(w_up, "replica", split_axis=2, concat_axis=1, tiled=True),
    )
    input_rows = jnp.einsum(
        "shf,hfd->sd", all_gate_act, rows_gate, preferred_element_type=jnp.float32
    )
    input_rows = input_rows + jnp.einsum(
        "shf,hfd->sd", all_up_act, rows_up, preferred_element_type=jnp.float32
    )
    grads_back = lax.all_to_all(
        input_rows.astype(jnp.bfloat16).reshape(experts_axis, capacity, slice_width),
        "expert",
        split_axis=0,
        concat_axis=0,
        tiled=True,
    ).reshape(slot_count, slice_width)
    token_grad = jnp.sum(
        grads_back[target].astype(jnp.float32).reshape(tok_rows, top_count, slice_width), axis=1
    ).astype(jnp.bfloat16)
    keep_gate, give_gate = pick_half(parity_bit, gate_local, 0)
    keep_up, give_up = pick_half(parity_bit, up_local, 0)
    keep_down, give_down = pick_half(parity_bit, down_local.reshape(2, -1, slice_width), 0)
    received = (
        partner_2(give_gate.astype(jnp.bfloat16), "expert", 0).astype(give_gate.dtype),
        partner_2(give_up.astype(jnp.bfloat16), "expert", 0).astype(give_up.dtype),
        partner_2(give_down.astype(jnp.bfloat16), "expert", 0).astype(give_down.dtype),
    )
    gate_grad = (keep_gate + received[0]).astype(jnp.bfloat16)[None]
    up_grad = (keep_up + received[1]).astype(jnp.bfloat16)[None]
    down_grad = (keep_down + received[2]).astype(jnp.bfloat16)[None]
    return (moe_out, token_grad, gate_grad, up_grad, down_grad)


def dot(left, right, dims):
    return lax.dot_general(left, right, (dims, ((), ())), preferred_element_type=F32)


def gate_column(place, tables):
    table = jnp.concatenate([ref[:, -LANES:] for ref in tables], axis=0).astype(F32)
    lane = lax.broadcasted_iota(jnp.int32, table.shape, 1)
    count = place[3]
    mine = (lane == place[2]) | (lane == place[2] + count) | (lane == place[2] + 2 * count)
    return jnp.sum(jnp.where(mine, table, 0.0), axis=1, keepdims=True)


def columns(index, width):
    return pl.ds(pl.multiple_of(index * width, width), width)


def quarter(place, r_rel, c_rel, width):
    return columns((place[0] ^ r_rel) * 2 + (place[1] ^ c_rel), width)


def load_kernel(place, gate_hbm, up_hbm, down_hbm, gate, up, down, sems):
    copies = [pltpu.make_async_copy(source, target, sems.at[n])
              for n, (source, target) in enumerate(
                  ((down_hbm, down), (gate_hbm, gate), (up_hbm, up)))]
    for copy in copies:
        copy.start()
    for copy in copies:
        copy.wait()


def cotangent_kernel(place, og00, og01, og10, og11, down, keep, give):
    width, units = og10.shape[1], keep.shape[1]
    total = [None, None]
    for c_rel, parts in enumerate(((og00, og01), (og10, og11))):
        rows = jnp.concatenate([part[:, :width] for part in parts], axis=0)
        for r_rel in range(2):
            block = down[columns(place[0] ^ r_rel, units), columns(place[1] ^ c_rel, width)]
            term = dot(rows, block, ((1,), (1,)))
            total[r_rel] = term if total[r_rel] is None else total[r_rel] + term
    keep[...] = total[0]
    give[...] = total[1].astype(give.dtype)


def products(place, c_rel, x, gate, up):
    width = x[0].shape[1]
    a = b = None
    for r_rel in range(2):
        rows = jnp.concatenate([part[...] for part in x[2 * r_rel : 2 * r_rel + 2]], axis=0)
        where = quarter(place, r_rel, c_rel, width)
        term_a = dot(rows, gate[:, where], ((1,), (1,)))
        term_b = dot(rows, up[:, where], ((1,), (1,)))
        a = term_a if a is None else a + term_a
        b = term_b if b is None else b + term_b
    return a, b


def half_kernel(place, x00, x01, x10, x11, gate, up, a_out, b_out):
    a_out[...], b_out[...] = products(place, 0, (x00, x01, x10, x11), gate, up)


def hidden_kernel(place, a_in, b_in, x00, x01, x10, x11, t0, t1, gate, up, hidden, act, slope):
    a, b = products(place, 1, (x00, x01, x10, x11), gate, up)
    a, b = a + a_in[...], b + b_in[...]
    weight = gate_column(place, (t0, t1))
    sigma = jax.nn.sigmoid(a)
    silu = a * sigma
    hidden[...] = (weight * (silu * b)).astype(hidden.dtype)
    act[...] = weight * silu
    slope[...] = weight * (b * (sigma * (1.0 + a * (1.0 - sigma))))


def give_kernel(place, own, other, act, slope, gate, up, da_out, db_out, give):
    width = give.shape[2]
    dh = own[...] + other[...].astype(F32)
    da = (dh * slope[...]).astype(BF16)
    db = (dh * act[...]).astype(BF16)
    da_out[...] = da
    db_out[...] = db
    for r_rel in range(2):
        where = quarter(place, r_rel, 1, width)
        block = dot(da, gate[:, where], ((1,), (0,))) + dot(db, up[:, where], ((1,), (0,)))
        give[r_rel] = block.astype(give.dtype)


def keep_kernel(place, da, db, gate, up, keep):
    width = keep.shape[2]
    for r_rel in range(2):
        where = quarter(place, r_rel, 0, width)
        keep[r_rel] = dot(da[...], gate[:, where], ((1,), (0,))) + dot(
            db[...], up[:, where], ((1,), (0,))
        )


def output_kernel(place, own, other, down, keep, give):
    width, units = keep.shape[1], own.shape[1]
    for c_rel in range(2):
        where = columns(place[1] ^ c_rel, width)
        block = dot(own[...], down[columns(place[0], units), where], ((1,), (0,)))
        block = block + dot(other[...], down[columns(place[0] ^ 1, units), where], ((1,), (0,)))
        if c_rel == 0:
            keep[...] = block
        else:
            give[...] = block.astype(give.dtype)


def down_grad_kernel(place, own, other, og00, og01, og10, og11, down_grad, made, sems):
    width, units = og10.shape[1], own.shape[1]
    copies = []
    for c_rel, parts in enumerate(((og00, og01), (og10, og11))):
        rows = jnp.concatenate([part[:, :width] for part in parts], axis=0)
        for r_rel, hidden in ((0, own), (1, other)):
            n = len(copies)
            made[n] = dot(hidden[...], rows, ((0,), (0,))).astype(made.dtype)
            where = columns(place[0] ^ r_rel, units), columns(place[1] ^ c_rel, width)
            copies.append(pltpu.make_async_copy(made.at[n], down_grad.at[where], sems.at[n]))
            copies[n].start()
    for copy in copies:
        copy.wait()


def weight_grad_kernel(place, da, db, x000, x001, x010, x011, x100, x101, x110, x111,
                       gate_grad, up_grad, made, sems):
    width = x000.shape[1]
    copies = []
    for r_rel, c_rel, parts in ((0, 0, (x000, x001)), (0, 1, (x010, x011)),
                                (1, 0, (x100, x101)), (1, 1, (x110, x111))):
        rows = jnp.concatenate([part[...] for part in parts], axis=0)
        where = slice(None), quarter(place, r_rel, c_rel, width)
        for source, target in ((da, gate_grad), (db, up_grad)):
            n = len(copies)
            made[n] = dot(source[...], rows, ((0,), (0,))).astype(made.dtype)
            copies.append(pltpu.make_async_copy(made.at[n], target.at[where], sems.at[n]))
            copies[n].start()
    for copy in copies:
        copy.wait()


def call(kernel, place, operands, outs, flops, in_hbm=(), scratch=(), limit=24 << 20,
         out_hbm=False):
    moved = sum(x.size * x.dtype.itemsize for x in (*operands, *outs))
    vmem = pl.BlockSpec(memory_space=pltpu.VMEM)
    hbm = pl.BlockSpec(memory_space=pltpu.HBM)
    return pl.pallas_call(
        kernel,
        out_shape=list(outs),
        in_specs=[pl.BlockSpec(memory_space=pltpu.SMEM)]
        + [hbm if n in in_hbm else vmem for n in range(len(operands))],
        out_specs=[hbm if out_hbm else vmem] * len(outs),
        scratch_shapes=list(scratch),
        compiler_params=pltpu.CompilerParams(vmem_limit_bytes=limit),
        cost_estimate=pl.CostEstimate(flops=flops, bytes_accessed=moved, transcendentals=0),
    )(place, *operands)


def struct(shape, dtype):
    return jax.ShapeDtypeStruct(shape, dtype)


def swap(value, expert_bits, replica_bit=0):
    count, replicas = lax.axis_size("expert"), lax.axis_size("replica")
    flip = expert_bits * replicas + replica_bit
    if not replica_bit:
        return lax.ppermute(value, "expert", [(i, i ^ expert_bits) for i in range(count)])
    if not expert_bits:
        return lax.ppermute(value, "replica", [(i, i ^ flip) for i in range(replicas)])
    return lax.ppermute(
        value, ("expert", "replica"), [(i, i ^ flip) for i in range(count * replicas)]
    )


def dense_device(tokens, expert_ids, gate_values, gate_weight, up_weight, down_weight, out_grad):
    devices = lax.axis_size("expert")
    experts, far = devices // 2, devices // 4
    tok_rows, slice_width = tokens.shape
    half = slice_width // 2
    me = lax.axis_index("expert")
    core, replica = me % 2, lax.axis_index("replica")
    place = jnp.stack([replica, core, me // 2, jnp.int32(experts)]).astype(jnp.int32)
    gate, up, down = gate_weight[0], up_weight[0], down_weight[0]
    units, model_width = gate.shape

    def order(own, peer, axis):
        return jnp.where(
            core == 0,
            jnp.concatenate([own, peer], axis=axis),
            jnp.concatenate([peer, own], axis=axis),
        )

    routed = expert_ids[:, :, None] == jnp.arange(experts, dtype=jnp.int32)
    table = jnp.sum(jnp.where(routed, gate_values[:, :, None], 0.0), axis=1)
    parts = []
    for _ in range(3):
        part = lax.reduce_precision(table, 8, 7)
        parts.append(part.astype(BF16))
        table = table - part
    coded = jnp.concatenate(parts, axis=1)
    coded = jnp.pad(coded, ((0, 0), (0, -coded.shape[1] % LANES)))
    own = lax.optimization_barrier(jnp.concatenate([tokens, out_grad], axis=1))
    low = jnp.concatenate([own[:, :half], own[:, 2 * half : 3 * half], coded], axis=1)
    high = jnp.concatenate([own[:, half : 2 * half], own[:, 3 * half :], coded], axis=1)
    mine, theirs = jnp.where(core == 0, low, high), jnp.where(core == 0, high, low)
    gate, up, down = call(
        load_kernel, place, (gate, up, down),
        [struct(w.shape, w.dtype) for w in (gate, up, down)], 0, in_hbm=(0, 1, 2),         scratch=[pltpu.SemaphoreType.DMA((3,))],
    )
    block = order(mine, swap(theirs, 1), 0)
    got = {step: swap(block, 4 * step) for step in reversed(range(1, far))}
    blocks = [block] + [got[step] for step in range(1, far)]
    og_here = jnp.concatenate([part[:, half:] for part in blocks], axis=0)
    x_here = jnp.concatenate([part[:, :half] for part in blocks], axis=0)
    og_side = swap(og_here, 2)
    x_side = swap(x_here, 2)
    x_cross = swap(x_here, 2, 1)
    x_up = swap(x_here, 0, 1)
    og = [og_here, og_side,
          swap(og_here[:, :half], 1), swap(og_side[:, :half], 1)]
    x = [x_here, x_side, swap(x_here, 1), swap(x_side, 1),
         x_up, x_cross, swap(x_up, 1), swap(x_cross, 1)]
    side_rows = x_here.shape[0]
    all_rows = 2 * side_rows
    work = 2 * all_rows * units

    d_own, d_give = call(
        cotangent_kernel, place, (*og, down),
        (struct((all_rows, units), F32), struct((all_rows, units), BF16)),
        work * 2 * slice_width,
    )
    d_got = swap(d_give, 0, 1)
    of_units = struct((all_rows, units), F32)
    of_units_low = struct((all_rows, units), BF16)
    straight, crossed = (x[0], x[1], x[4], x[5]), (x[2], x[3], x[6], x[7])
    a_half, b_half = call(
        half_kernel, place, (*straight, gate, up), (of_units, of_units),
        work * model_width,
    )
    hidden, act, slope = call(
        hidden_kernel, place,
        (a_half, b_half, *crossed, og_here, og_side, gate, up),
        (of_units_low, of_units, of_units), work * model_width,
    )
    hidden_got = swap(hidden, 0, 1)
    da, db, dx_give = call(
        give_kernel, place, (d_own, d_got, act, slope, gate, up),
        (of_units_low, of_units_low, struct((2, all_rows, half), BF16)), work * model_width,
    )
    dx_got = swap(dx_give, 1)
    (dx_keep,) = call(
        keep_kernel, place, (da, db, gate, up),
        (struct((2, all_rows, half), F32),), work * model_width,
    )
    dx = dx_keep + dx_got.astype(F32)
    dx_cross = swap(dx[1, side_rows:].astype(BF16), 2, 1)
    dx_side = swap(dx[0, side_rows:].astype(BF16), 2)
    dx_up = swap(dx[1, :side_rows].astype(BF16), 0, 1)

    y_keep, y_give = call(
        output_kernel, place, (hidden, hidden_got, down),
        (struct((all_rows, half), F32), struct((all_rows, half), BF16)),
        work * 2 * slice_width,
    )
    y = y_keep + swap(y_give, 1).astype(F32)
    (down_grad,) = call(
        down_grad_kernel, place, (hidden, hidden_got, *og),
        (struct(down.shape, BF16),), work * 2 * slice_width, out_hbm=True,
        scratch=[pltpu.VMEM((4, units, half), BF16), pltpu.SemaphoreType.DMA((4,))],
    )
    gate_grad, up_grad = call(
        weight_grad_kernel, place, (da, db, *x),
        (struct(gate.shape, BF16), struct(up.shape, BF16)), work * 2 * model_width, out_hbm=True,
        scratch=[pltpu.VMEM((8, units, half), BF16), pltpu.SemaphoreType.DMA((8,))],
    )

    pair = 2 * tok_rows

    def far_sum(parts):
        got = [swap(parts[step].astype(BF16), 4 * step) for step in reversed(range(1, far))]
        return sum((value.astype(F32) for value in got), parts[0])

    def rows_of(value, step):
        return value[step * pair : (step + 1) * pair]

    y_pair = far_sum([
        jnp.concatenate([rows_of(y, step), rows_of(y, far + step)], axis=0) for step in range(far)
    ])
    y_sum = y_pair[:pair] + swap(y_pair[pair:].astype(BF16), 2).astype(F32)
    dx_near = (dx[0, :side_rows] + dx_side.astype(F32)) + (
        dx_up.astype(F32) + dx_cross.astype(F32)
    )
    dx_sum = far_sum([rows_of(dx_near, step) for step in range(far)])
    total = jnp.concatenate([y_sum, dx_sum], axis=1).astype(BF16)
    first, second = total[:tok_rows], total[tok_rows:]
    kept = jnp.where(core == 0, first, second)
    got = swap(jnp.where(core == 0, second, first), 1)
    moe_out = order(kept[:, :half], got[:, :half], 1)
    token_grad = order(kept[:, half:], got[:, half:], 1)
    return moe_out, token_grad, gate_grad[None], up_grad[None], down_grad[None]


def per_device(tokens, expert_ids, gate_values, gate_weight, up_weight, down_weight, out_grad):
    args = (tokens, expert_ids, gate_values, gate_weight, up_weight, down_weight, out_grad)
    devices, replicas = lax.axis_size("expert"), lax.axis_size("replica")
    every_expert = expert_ids.shape[1] == devices // 2
    power = devices & (devices - 1) == 0 and devices >= 4 and 3 * (devices // 2) <= LANES
    aligned = tokens.shape[1] % (2 * LANES) == 0 and gate_weight.shape[1] % LANES == 0
    if every_expert and power and replicas == 2 and aligned:
        return dense_device(*args)
    return routed_device(*args)


def solution(mesh):
    placed = (
        P("expert", "replica"),
        P("expert", None),
        P("expert", None),
        P("expert", "replica", None),
        P("expert", "replica", None),
        P("expert", None, "replica"),
        P("expert", "replica"),
    )
    return jax.shard_map(
        per_device,
        mesh=mesh,
        in_specs=placed,
        out_specs=(
            P("expert", "replica"),
            P("expert", "replica"),
            P("expert", "replica", None),
            P("expert", "replica", None),
            P("expert", None, "replica"),
        ),
        check_vma=False,
    )
```
